32 devices in a mesh: replica: 8 (over y, x, core), tensor: 4 (over z).
Axes of the slice: x: 2, y: 2, z: 4, core: 2. Of those that a mesh axis runs over, the one named last changes fastest.
Arguments:
- inputs: bfloat16 [4096, 4096], P('replica', 'tensor'), may hold values from -6 to 6
- out_grad: bfloat16 [4096, 2560], P(('replica', 'tensor')), may hold values from -6 to 6
- weight: bfloat16 [4096, 2560], P('tensor'), may hold values from -0.09375 to 0.09375
- momentum: bfloat16 [8, 4096, 2560], P('replica', 'tensor'), may hold values from -6 to 6
- selected: int32 [2560, 64], P('tensor'), may hold values from 0 to 4095, as said below
Outputs:
- input_grad: bfloat16 [4096, 4096], P('replica', 'tensor')
- new_momentum: bfloat16 [8, 4096, 2560], P('replica', 'tensor')
- update: bfloat16 [4096, 2560], P('tensor')
The draws below stay inside these ranges and needn't reach their ends.
Inputs may be any that keep to these rules, and one draw needn't show every extreme that they name: `selected`: each row holds 64 different frequency numbers u * 64 + v of one block; the same selection holds for every replica.
All inputs are finite; a program needn't handle non-finite values.
Results may differ from the reference program's by a relative error of at most 0.001.
Values may be sent and summed in bfloat16 or wider, within the bound.
A program may use at most 192 MiB of HBM per device.

```python
import math
import jax
import jax.numpy as jnp
from jax import lax

HQW = 4096
DW = 2560
BLK = 64
TOPK = 64
TOKR = 512
TOKENS = 4096
NBLK = 2560
N_REPLICA = 8


def draw_selected(key, part):
    scores = jax.random.randint(key, (NBLK, BLK * BLK), 0, 2 ** 18) * (BLK * BLK) + jnp.arange(BLK * BLK, dtype=jnp.int32)[None, :]
    unused, chosen = lax.top_k(scores, TOPK)
    return chosen.astype(jnp.int32)


def block_levels(rng, extent, cuts, smallest, top_value):
    level = 1.0
    for axis_at, parts in cuts:
        steps = jax.random.uniform(jax.random.fold_in(jax.random.fold_in(rng, 6), axis_at), (parts,), jnp.float32, smallest / len(cuts), top_value / len(cuts))
        level = level * jnp.repeat(jnp.exp(steps), extent[axis_at] // parts).reshape((-1,) + (1,) * (len(extent) - 1 - axis_at))
    return level


def noise(own_key, dims, spread, limit, cuts=(), kind=jnp.bfloat16):
    result = jax.random.normal(own_key, dims, jnp.float32) * spread
    if len(cuts) > 0:
        result = block_levels(own_key, dims, cuts, -0.22, 0.18) * result
    return jnp.clip(result, min=-limit, max=limit).astype(kind)


def setup_inputs(seed: int = 0) -> dict:
    key_list = jax.random.split(jax.random.key(seed), 6)
    inputs = noise(key_list[0], (TOKENS, HQW), 1.0, 6.0, ((0, 8), (1, 4)))
    out_grad = noise(key_list[1], (TOKENS, DW), 1.0, 6.0, ((0, 32),))
    weight = noise(key_list[2], (HQW, DW), HQW ** -0.5, 0.09375, ((0, 4),))
    momentum = noise(key_list[3], (N_REPLICA, HQW, DW), 1.0, 6.0, ((0, 8), (1, 4)))
    selected = draw_selected(jax.random.fold_in(key_list[5], 71), 0)
    return dict(inputs=inputs, out_grad=out_grad, weight=weight, momentum=momentum, selected=selected)


HIGH = lax.Precision.HIGHEST

def basis_rows(freq):
    place = jnp.arange(BLK, dtype=jnp.float32)
    angle = math.pi * (2.0 * place + 1.0) / (2.0 * BLK)
    fvals = freq.astype(jnp.float32)[..., None]
    table = jnp.cos(fvals * angle) * math.sqrt(2.0 / BLK)
    return jnp.where(fvals == 0.0, math.sqrt(1.0 / BLK), table)

def bases(selected, rows, cols):
    row_basis = basis_rows(selected // BLK).reshape(rows // BLK, cols // BLK, TOPK, BLK)
    col_basis = basis_rows(selected % BLK).reshape(rows // BLK, cols // BLK, TOPK, BLK)
    return (row_basis, col_basis)

def encode_sel(matrix, row_basis, col_basis):
    grid = row_basis.shape
    split = matrix.reshape(grid[0], BLK, grid[1], BLK)
    proj = jnp.einsum('rcki,ricj->rckj', row_basis, split, precision=HIGH)
    return lax.optimization_barrier(jnp.sum(proj * col_basis, axis=-1)).reshape(grid[0] * grid[1], TOPK)

def decode_sel(values, row_basis, col_basis):
    grid = row_basis.shape
    weighted = col_basis * values.reshape(grid[0], grid[1], TOPK)[..., None]
    blocks = jnp.einsum('rcki,rckj->ricj', row_basis, weighted, precision=HIGH)
    return blocks.reshape(grid[0] * BLK, grid[1] * BLK)

def reference(inputs, out_grad, weight, momentum, selected):
    rows, cols = weight.shape
    row_basis, col_basis = bases(selected, rows, cols)
    scale = 1.0 / math.sqrt(TOKR)
    xs = inputs.reshape(N_REPLICA, TOKR, rows)
    gs = out_grad.reshape(N_REPLICA, TOKR, cols)

    def replica_step(items):
        acts, grads, moment = items
        wgrad = lax.dot_general(acts, grads, (((0,), (0,)), ((), ())), preferred_element_type=jnp.float32) * scale
        dacts = lax.dot_general(grads, weight, (((1,), (1,)), ((), ())), preferred_element_type=jnp.float32)
        accum = 0.999 * moment.astype(jnp.float32) + wgrad
        picked = encode_sel(accum, row_basis, col_basis)
        fresh = accum - decode_sel(picked, row_basis, col_basis)
        return (dacts.astype(jnp.bfloat16), fresh.astype(jnp.bfloat16), picked)
    dacts, fresh, picked = lax.map(replica_step, (xs, gs, momentum))
    mean_sent = lax.optimization_barrier(jnp.mean(picked, axis=0))
    update = BLK / math.sqrt(TOPK) * decode_sel(mean_sent, row_basis, col_basis)
    return (dacts.reshape(TOKENS, rows), fresh, update.astype(jnp.bfloat16))
```

```python
import functools
import math

import jax
import jax.numpy as jnp
import numpy as np
from jax import lax
from jax.experimental import pallas as pl
from jax.experimental.pallas import tpu as pltpu
from jax.sharding import PartitionSpec as P

BLK = 64
TOPK = 64
LANES = 2 * BLK
WIDE = 256


def dct_table():
    place = np.arange(BLK)[:, None]
    freq = np.arange(BLK)[None, :]
    table = np.cos(math.pi * (2.0 * place + 1.0) * freq / (2.0 * BLK)) * math.sqrt(2.0 / BLK)
    table[:, 0] = math.sqrt(1.0 / BLK)
    return np.concatenate([table, table], axis=1).astype(np.float32)


def split(x):
    high = x.astype(jnp.bfloat16)
    low = (x - high.astype(jnp.float32)).astype(jnp.bfloat16)
    return high, low


def bases(picks, table):
    rows_at = jnp.broadcast_to(lax.shift_right_logical(picks, 6), (BLK, LANES))
    cols_at = jnp.broadcast_to(picks & (BLK - 1), (BLK, LANES))
    row_basis = jnp.take_along_axis(table, rows_at, axis=1)
    col_basis = jnp.take_along_axis(table, cols_at, axis=1)
    first = lax.broadcasted_iota(jnp.int32, (BLK, LANES), 1) < BLK
    diagonal = jnp.concatenate(
        [jnp.where(first, col_basis, 0.0), jnp.where(first, 0.0, col_basis)], axis=0
    )
    return row_basis, split(diagonal)


def encode(block, row_basis, diagonal):
    high, low = split(block)
    dhigh, dlow = diagonal
    both = jnp.concatenate([dhigh, dlow], axis=1)
    part = jnp.dot(
        jnp.concatenate([high, low], axis=1),
        jnp.concatenate([both, both], axis=0),
        preferred_element_type=jnp.float32,
    )
    proj = part[:, :LANES] + part[:, LANES:]
    return jnp.sum(row_basis * proj, axis=0, keepdims=True)


def decode(values, row_basis, diagonal):
    high, low = split(row_basis * values)
    dhigh, dlow = diagonal
    both = jnp.concatenate([dhigh, dlow], axis=0)
    part = lax.dot_general(
        jnp.concatenate([high, low], axis=1),
        jnp.concatenate([both, both], axis=1),
        (((1,), (1,)), ((), ())),
        preferred_element_type=jnp.float32,
    )
    return part[:, :LANES] + part[:, LANES:]


def group_of(strips):
    return 8 if strips % 8 == 0 else strips


def momentum_kernel(scale, strips, x_ref, g_ref, m_ref, sel_ref, table_ref, fresh_ref, sent_ref, acc_ref):
    acc_ref[...] = (
        jnp.dot(x_ref[...], g_ref[...], preferred_element_type=jnp.float32) * scale
        + 0.999 * m_ref[...].astype(jnp.float32)
    )
    table = table_ref[...]

    some = group_of(strips)

    @pl.loop(0, strips // some)
    def _(group):
        near = pl.ds(pl.multiple_of(group * some, some), some)
        for pair in range(WIDE // LANES):
            lanes = pl.ds(pair * LANES, LANES)
            picks = sel_ref[0, near, lanes]
            found = []
            for one in range(some):
                at = pl.ds(pl.multiple_of((group * some + one) * BLK, BLK), BLK)
                row_basis, diagonal = bases(picks[one : one + 1], table)
                block = acc_ref[at, lanes]
                values = encode(block, row_basis, diagonal)
                found.append(values)
                fresh_ref[at, lanes] = (block - decode(values, row_basis, diagonal)).astype(jnp.bfloat16)
            sent_ref[0, near, lanes] = jnp.concatenate(found, axis=0)


def update_kernel(strips, mean_ref, sel_ref, table_ref, update_ref):
    table = table_ref[...]

    some = group_of(strips)

    @pl.loop(0, strips // some)
    def _(group):
        near = pl.ds(pl.multiple_of(group * some, some), some)
        for pair in range(WIDE // LANES):
            lanes = pl.ds(pair * LANES, LANES)
            picks = sel_ref[0, near, lanes]
            means = mean_ref[0, near, lanes] * (BLK / math.sqrt(TOPK))
            for one in range(some):
                at = pl.ds(pl.multiple_of((group * some + one) * BLK, BLK), BLK)
                row_basis, diagonal = bases(picks[one : one + 1], table)
                update_ref[at, lanes] = decode(means[one : one + 1], row_basis, diagonal).astype(jnp.bfloat16)


def body(inputs, out_grad, weight, momentum, selected):
    rows, cols = weight.shape
    tokens = inputs.shape[0]
    scale = 1.0 / math.sqrt(tokens)
    strips, steps = rows // BLK, cols // WIDE
    table = jnp.asarray(dct_table())
    gathered = lax.all_gather(out_grad, "tensor", axis=0, tiled=True)
    turned = inputs.T
    picks = selected.reshape(strips, steps, WIDE).swapaxes(0, 1)

    small = pl.BlockSpec((1, strips, WIDE), lambda c: (c, 0, 0))
    whole_table = pl.BlockSpec((BLK, LANES), lambda c: (0, 0))
    tall = pl.BlockSpec((rows, WIDE), lambda c: (0, c))
    fresh, sent = pl.pallas_call(
        functools.partial(momentum_kernel, scale, strips),
        grid=(steps,),
        out_shape=(
            jax.ShapeDtypeStruct((rows, cols), jnp.bfloat16),
            jax.ShapeDtypeStruct((steps, strips, WIDE), jnp.float32),
        ),
        in_specs=[
            pl.BlockSpec((rows, tokens), lambda c: (0, 0)),
            pl.BlockSpec((tokens, WIDE), lambda c: (0, c)),
            tall,
            small,
            whole_table,
        ],
        out_specs=(tall, small),
        scratch_shapes=[pltpu.VMEM((rows, WIDE), jnp.float32)],
        cost_estimate=pl.CostEstimate(
            flops=2 * rows * cols * (tokens + 512), bytes_accessed=8 * rows * cols, transcendentals=0
        ),
        name="momentum_step",
    )(turned, gathered, momentum[0], picks, table)
    mean_sent = lax.psum(sent, "replica") / lax.axis_size("replica")
    dacts = lax.dot_general(
        gathered, weight, (((1,), (1,)), ((), ())), preferred_element_type=jnp.float32
    ).astype(jnp.bfloat16)
    update = pl.pallas_call(
        functools.partial(update_kernel, strips),
        grid=(steps,),
        out_shape=jax.ShapeDtypeStruct((rows, cols), jnp.bfloat16),
        in_specs=[small, small, whole_table],
        out_specs=tall,
        cost_estimate=pl.CostEstimate(
            flops=2 * rows * cols * 256, bytes_accessed=2 * rows * cols, transcendentals=0
        ),
        name="update_step",
    )(mean_sent, picks, table)
    return dacts, fresh[None], update


def solution(mesh):
    return jax.shard_map(
        body,
        mesh=mesh,
        in_specs=(
            P("replica", "tensor"),
            P(("replica", "tensor"), None),
            P("tensor", None),
            P("replica", "tensor", None),
            P("tensor", None),
        ),
        out_specs=(P("replica", "tensor"), P("replica", "tensor", None), P("tensor", None)),
        check_vma=False,
    )
```

```python
import functools
import math

import jax
import jax.numpy as jnp
import numpy as np
from jax import lax
from jax.experimental import pallas as pl
from jax.experimental.pallas import tpu as pltpu
from jax.sharding import PartitionSpec as P

BLK = 64
TOPK = 64
LANES = 2 * BLK
WIDE = 256


def dct_table():
    place = np.arange(BLK)[:, None]
    freq = np.arange(BLK)[None, :]
    table = np.cos(math.pi * (2.0 * place + 1.0) * freq / (2.0 * BLK)) * math.sqrt(2.0 / BLK)
    table[:, 0] = math.sqrt(1.0 / BLK)
    return np.concatenate([table, table], axis=1).astype(np.float32)


def split(x):
    high = x.astype(jnp.bfloat16)
    low = (x - high.astype(jnp.float32)).astype(jnp.bfloat16)
    return high, low


def bases(picks, table):
    rows_at = jnp.broadcast_to(lax.shift_right_logical(picks, 6), (BLK, LANES))
    cols_at = jnp.broadcast_to(picks & (BLK - 1), (BLK, LANES))
    row_basis = jnp.take_along_axis(table, rows_at, axis=1)
    col_basis = jnp.take_along_axis(table, cols_at, axis=1)
    first = lax.broadcasted_iota(jnp.int32, (BLK, LANES), 1) < BLK
    diagonal = jnp.concatenate(
        [jnp.where(first, col_basis, 0.0), jnp.where(first, 0.0, col_basis)], axis=0
    )
    return row_basis, split(diagonal)


def encode(block, row_basis, diagonal):
    high, low = split(block)
    dhigh, dlow = diagonal
    part = jnp.dot(
        jnp.concatenate([high, low], axis=0),
        jnp.concatenate([dhigh, dlow], axis=1),
        preferred_element_type=jnp.float32,
    )
    proj = part[:BLK, :LANES] + (part[:BLK, LANES:] + part[BLK:, :LANES])
    return jnp.sum(row_basis * proj, axis=0, keepdims=True)


def decode(values, row_basis, diagonal):
    high, low = split(row_basis * values)
    dhigh, dlow = diagonal
    part = lax.dot_general(
        jnp.concatenate([high, low], axis=0),
        jnp.concatenate([dhigh, dlow], axis=0),
        (((1,), (1,)), ((), ())),
        preferred_element_type=jnp.float32,
    )
    return part[:BLK, :LANES] + (part[:BLK, LANES:] + part[BLK:, :LANES])


def group_of(strips):
    return 8 if strips % 8 == 0 else strips


def momentum_kernel(scale, strips, x_ref, g_ref, m_ref, sel_ref, table_ref, fresh_ref, sent_ref, acc_ref):
    acc_ref[...] = (
        jnp.dot(x_ref[...], g_ref[...], preferred_element_type=jnp.float32) * scale
        + 0.999 * m_ref[...].astype(jnp.float32)
    )
    table = table_ref[...]

    some = group_of(strips)

    @pl.loop(0, strips // some)
    def _(group):
        near = pl.ds(pl.multiple_of(group * some, some), some)
        for pair in range(WIDE // LANES):
            lanes = pl.ds(pair * LANES, LANES)
            picks = sel_ref[pair, near]
            found = []
            for one in range(some):
                at = pl.ds(pl.multiple_of((group * some + one) * BLK, BLK), BLK)
                row_basis, diagonal = bases(picks[one : one + 1], table)
                block = acc_ref[at, lanes]
                values = encode(block, row_basis, diagonal)
                found.append(values)
                fresh_ref[at, lanes] = (block - decode(values, row_basis, diagonal)).astype(jnp.bfloat16)
            sent_ref[pair, near] = jnp.concatenate(found, axis=0)


def update_kernel(strips, mean_ref, sel_ref, table_ref, update_ref):
    table = table_ref[...]

    some = group_of(strips)

    @pl.loop(0, strips // some)
    def _(group):
        near = pl.ds(pl.multiple_of(group * some, some), some)
        for pair in range(WIDE // LANES):
            lanes = pl.ds(pair * LANES, LANES)
            picks = sel_ref[pair, near]
            means = mean_ref[pair, near] * (BLK / math.sqrt(TOPK))
            for one in range(some):
                at = pl.ds(pl.multiple_of((group * some + one) * BLK, BLK), BLK)
                row_basis, diagonal = bases(picks[one : one + 1], table)
                update_ref[at, lanes] = decode(means[one : one + 1], row_basis, diagonal).astype(jnp.bfloat16)


def greet(axis, n):
    me = lax.axis_index(axis)
    barrier = pltpu.get_barrier_semaphore()
    for step in range(1, n):
        pl.semaphore_signal(
            barrier, inc=1, device_id={axis: lax.rem(me + step, n)}, device_id_type=pl.DeviceIdType.MESH
        )
    pl.semaphore_wait(barrier, n - 1)
    return me


def gather_kernel(axis, n, own_ref, all_ref, send_sem, recv_sem, own_sem):
    me = greet(axis, n)
    depth = own_ref.shape[0]
    place = all_ref.at[pl.ds(pl.multiple_of(me * depth, depth), depth)]
    copies = [
        pltpu.make_async_remote_copy(
            src_ref=own_ref,
            dst_ref=place,
            send_sem=send_sem.at[step],
            recv_sem=recv_sem.at[step],
            device_id={axis: lax.rem(me + step, n)},
            device_id_type=pl.DeviceIdType.MESH,
        )
        for step in range(1, n)
    ]
    for copy in copies:
        copy.start()
    own = pltpu.make_async_copy(own_ref, place, own_sem)
    own.start()
    own.wait()
    for copy in copies:
        copy.wait()


def mean_kernel(axis, n, sent_ref, mean_ref, parts, total, send_sem, recv_sem, back_sem, give_sem):
    me = greet(axis, n)
    scatter = []
    spread = []
    for step in range(1, n):
        peer = lax.rem(me + step, n)
        scatter.append(
            pltpu.make_async_remote_copy(
                src_ref=sent_ref.at[peer],
                dst_ref=parts.at[step],
                send_sem=send_sem.at[step],
                recv_sem=recv_sem.at[step],
                device_id={axis: peer},
                device_id_type=pl.DeviceIdType.MESH,
            )
        )
        spread.append(
            pltpu.make_async_remote_copy(
                src_ref=total,
                dst_ref=mean_ref.at[me],
                send_sem=back_sem.at[step],
                recv_sem=give_sem.at[step],
                device_id={axis: peer},
                device_id_type=pl.DeviceIdType.MESH,
            )
        )
    for copy in scatter:
        copy.start()
    value = sent_ref[me]
    for step, copy in enumerate(scatter, 1):
        copy.wait_recv()
        value = value + parts[step]
    total[...] = value / n
    for copy in spread:
        copy.start()
    mean_ref[me] = total[...]
    for copy in scatter:
        copy.wait_send()
    for copy in spread:
        copy.wait()


def gather_rows(array, axis):
    n = lax.axis_size(axis)
    depth, cols = array.shape
    return pl.pallas_call(
        functools.partial(gather_kernel, axis, n),
        out_shape=jax.ShapeDtypeStruct((n * depth, cols), array.dtype),
        in_specs=[pl.BlockSpec(memory_space=pltpu.VMEM)],
        out_specs=pl.BlockSpec(memory_space=pl.ANY),
        scratch_shapes=[
            pltpu.SemaphoreType.DMA((n,)),
            pltpu.SemaphoreType.DMA((n,)),
            pltpu.SemaphoreType.DMA,
        ],
        compiler_params=pltpu.CompilerParams(collective_id=0, has_side_effects=True),
        name="gather_rows",
    )(array)


def mean_over(array, axis):
    n = lax.axis_size(axis)
    lanes = array.shape[-1]
    slices = array.reshape(n, -1, lanes)
    mean = pl.pallas_call(
        functools.partial(mean_kernel, axis, n),
        out_shape=jax.ShapeDtypeStruct(slices.shape, jnp.float32),
        in_specs=[pl.BlockSpec(memory_space=pltpu.VMEM)],
        out_specs=pl.BlockSpec(memory_space=pltpu.VMEM),
        scratch_shapes=[
            pltpu.VMEM(slices.shape, jnp.float32),
            pltpu.VMEM(slices.shape[1:], jnp.float32),
        ]
        + [pltpu.SemaphoreType.DMA((n,))] * 4,
        compiler_params=pltpu.CompilerParams(collective_id=1, has_side_effects=True),
        name="mean_over",
    )(slices)
    return mean.reshape(array.shape)


def body(inputs, out_grad, weight, momentum, selected):
    rows, cols = weight.shape
    tokens = inputs.shape[0]
    scale = 1.0 / math.sqrt(tokens)
    strips, steps = rows // BLK, cols // WIDE
    table = jnp.asarray(dct_table())
    gathered = gather_rows(out_grad, "tensor")
    turned = inputs.T
    picks = selected.reshape(strips, cols // LANES, LANES).swapaxes(0, 1)

    small = pl.BlockSpec((WIDE // LANES, strips, LANES), lambda c: (c, 0, 0))
    whole_table = pl.BlockSpec((BLK, LANES), lambda c: (0, 0))
    tall = pl.BlockSpec((rows, WIDE), lambda c: (0, c))
    fresh, sent = pl.pallas_call(
        functools.partial(momentum_kernel, scale, strips),
        grid=(steps,),
        out_shape=(
            jax.ShapeDtypeStruct((rows, cols), jnp.bfloat16),
            jax.ShapeDtypeStruct((cols // LANES, strips, LANES), jnp.float32),
        ),
        in_specs=[
            pl.BlockSpec((rows, tokens), lambda c: (0, 0)),
            pl.BlockSpec((tokens, WIDE), lambda c: (0, c)),
            tall,
            small,
            whole_table,
        ],
        out_specs=(tall, small),
        scratch_shapes=[pltpu.VMEM((rows, WIDE), jnp.float32)],
        cost_estimate=pl.CostEstimate(
            flops=2 * rows * cols * (tokens + 512), bytes_accessed=8 * rows * cols, transcendentals=0
        ),
        name="momentum_step",
    )(turned, gathered, momentum[0], picks, table)
    mean_sent = mean_over(sent, "replica")
    dacts = lax.dot_general(
        gathered, weight, (((1,), (1,)), ((), ())), preferred_element_type=jnp.float32
    ).astype(jnp.bfloat16)
    update = pl.pallas_call(
        functools.partial(update_kernel, strips),
        grid=(steps,),
        out_shape=jax.ShapeDtypeStruct((rows, cols), jnp.bfloat16),
        in_specs=[small, small, whole_table],
        out_specs=tall,
        cost_estimate=pl.CostEstimate(
            flops=2 * rows * cols * 256, bytes_accessed=2 * rows * cols, transcendentals=0
        ),
        name="update_step",
    )(mean_sent, picks, table)
    return dacts, fresh[None], update


def solution(mesh):
    return jax.shard_map(
        body,
        mesh=mesh,
        in_specs=(
            P("replica", "tensor"),
            P(("replica", "tensor"), None),
            P("tensor", None),
            P("replica", "tensor", None),
            P("tensor", None),
        ),
        out_specs=(P("replica", "tensor"), P("replica", "tensor", None), P("tensor", None)),
        check_vma=False,
    )
```

```python
import functools
import math

import jax
import jax.numpy as jnp
import numpy as np
from jax import lax
from jax.experimental import pallas as pl
from jax.experimental.pallas import tpu as pltpu
from jax.sharding import PartitionSpec as P

BLK = 64
TOPK = 64
LANES = 2 * BLK
WIDE = 256
PIECES = 2


def dct_table():
    place = np.arange(BLK)[:, None]
    freq = np.arange(BLK)[None, :]
    table = np.cos(math.pi * (2.0 * place + 1.0) * freq / (2.0 * BLK)) * math.sqrt(2.0 / BLK)
    table[:, 0] = math.sqrt(1.0 / BLK)
    return np.concatenate([table, table], axis=1).astype(np.float32)


def split(x):
    high = x.astype(jnp.bfloat16)
    low = (x - high.astype(jnp.float32)).astype(jnp.bfloat16)
    return high, low


def bases(picks, table):
    rows_at = jnp.broadcast_to(lax.shift_right_logical(picks, 6), (BLK, LANES))
    cols_at = jnp.broadcast_to(picks & (BLK - 1), (BLK, LANES))
    row_basis = jnp.take_along_axis(table, rows_at, axis=1)
    col_basis = jnp.take_along_axis(table, cols_at, axis=1)
    first = lax.broadcasted_iota(jnp.int32, (BLK, LANES), 1) < BLK
    diagonal = jnp.concatenate(
        [jnp.where(first, col_basis, 0.0), jnp.where(first, 0.0, col_basis)], axis=0
    )
    return row_basis, split(diagonal)


def encode(block, row_basis, diagonal):
    high, low = split(block)
    dhigh, dlow = diagonal
    part = jnp.dot(
        jnp.concatenate([high, low], axis=0),
        jnp.concatenate([dhigh, dlow], axis=1),
        preferred_element_type=jnp.float32,
    )
    proj = part[:BLK, :LANES] + (part[:BLK, LANES:] + part[BLK:, :LANES])
    return jnp.sum(row_basis * proj, axis=0, keepdims=True)


def decode(values, row_basis, diagonal):
    high, low = split(row_basis * values)
    dhigh, dlow = diagonal
    part = lax.dot_general(
        jnp.concatenate([high, low], axis=0),
        jnp.concatenate([dhigh, dlow], axis=0),
        (((1,), (1,)), ((), ())),
        preferred_element_type=jnp.float32,
    )
    return part[:BLK, :LANES] + (part[:BLK, LANES:] + part[BLK:, :LANES])


def group_of(strips):
    return 8 if strips % 8 == 0 else strips


def momentum_kernel(scale, strips, x_ref, g_ref, m_ref, sel_ref, table_ref, fresh_ref, sent_ref, acc_ref):
    acc_ref[...] = (
        jnp.dot(x_ref[...], g_ref[...], preferred_element_type=jnp.float32) * scale
        + 0.999 * m_ref[...].astype(jnp.float32)
    )
    table = table_ref[...]

    some = group_of(strips)

    @pl.loop(0, strips // some)
    def _(group):
        near = pl.ds(pl.multiple_of(group * some, some), some)
        for pair in range(WIDE // LANES):
            lanes = pl.ds(pair * LANES, LANES)
            picks = sel_ref[pair, near]
            found = []
            for one in range(some):
                at = pl.ds(pl.multiple_of((group * some + one) * BLK, BLK), BLK)
                row_basis, diagonal = bases(picks[one : one + 1], table)
                block = acc_ref[at, lanes]
                values = encode(block, row_basis, diagonal)
                found.append(values)
                fresh_ref[at, lanes] = (block - decode(values, row_basis, diagonal)).astype(jnp.bfloat16)
            sent_ref[pair, near] = jnp.concatenate(found, axis=0)


def update_kernel(strips, mean_ref, sel_ref, table_ref, update_ref):
    table = table_ref[...]

    some = group_of(strips)

    @pl.loop(0, strips // some)
    def _(group):
        near = pl.ds(pl.multiple_of(group * some, some), some)
        for pair in range(WIDE // LANES):
            lanes = pl.ds(pair * LANES, LANES)
            picks = sel_ref[pair, near]
            means = mean_ref[pair, near] * (BLK / math.sqrt(TOPK))
            for one in range(some):
                at = pl.ds(pl.multiple_of((group * some + one) * BLK, BLK), BLK)
                row_basis, diagonal = bases(picks[one : one + 1], table)
                update_ref[at, lanes] = decode(means[one : one + 1], row_basis, diagonal).astype(jnp.bfloat16)


def greet(axis, n):
    me = lax.axis_index(axis)
    barrier = pltpu.get_barrier_semaphore()
    for step in range(1, n):
        pl.semaphore_signal(
            barrier, inc=1, device_id={axis: lax.rem(me + step, n)}, device_id_type=pl.DeviceIdType.MESH
        )
    pl.semaphore_wait(barrier, n - 1)
    return me


def gather_kernel(axis, n, own_ref, all_ref, send_sem, recv_sem, own_sem):
    me = lax.axis_index(axis)
    right, left = lax.rem(me + 1, n), lax.rem(me + n - 1, n)
    barrier = pltpu.get_barrier_semaphore()
    for peer in (left, right):
        pl.semaphore_signal(barrier, inc=1, device_id={axis: peer}, device_id_type=pl.DeviceIdType.MESH)
    pl.semaphore_wait(barrier, 2)
    depth, cols = own_ref.shape
    width = cols // (2 * PIECES)

    def rows_of(owner):
        return pl.ds(pl.multiple_of(owner * depth, depth), depth)

    def hop(step, piece, way):
        owner = lax.rem(me + n - step, n) if way == 0 else lax.rem(me + step, n)
        lanes = pl.ds((way * PIECES + piece) * width, width)
        there = all_ref.at[rows_of(owner), lanes]
        return pltpu.make_async_remote_copy(
            src_ref=own_ref.at[:, lanes] if step == 0 else there,
            dst_ref=there,
            send_sem=send_sem.at[step, way * PIECES + piece],
            recv_sem=recv_sem.at[step, way * PIECES + piece],
            device_id={axis: right if way == 0 else left},
            device_id_type=pl.DeviceIdType.MESH,
        )

    hops = [[hop(step, piece, way) for piece in range(PIECES) for way in range(2)] for step in range(n - 1)]
    for copy in hops[0]:
        copy.start()
    own = pltpu.make_async_copy(own_ref, all_ref.at[rows_of(me)], own_sem)
    own.start()
    for step in range(n - 1):
        for at, copy in enumerate(hops[step]):
            copy.wait_recv()
            if step + 1 < n - 1:
                hops[step + 1][at].start()
    own.wait()
    for some in hops:
        for copy in some:
            copy.wait_send()


def mean_kernel(axis, n, sent_ref, mean_ref, parts, total, send_sem, recv_sem, back_sem, give_sem):
    me = greet(axis, n)
    scatter = []
    spread = []
    for step in range(1, n):
        peer = lax.rem(me + step, n)
        scatter.append(
            pltpu.make_async_remote_copy(
                src_ref=sent_ref.at[peer],
                dst_ref=parts.at[step],
                send_sem=send_sem.at[step],
                recv_sem=recv_sem.at[step],
                device_id={axis: peer},
                device_id_type=pl.DeviceIdType.MESH,
            )
        )
        spread.append(
            pltpu.make_async_remote_copy(
                src_ref=total,
                dst_ref=mean_ref.at[me],
                send_sem=back_sem.at[step],
                recv_sem=give_sem.at[step],
                device_id={axis: peer},
                device_id_type=pl.DeviceIdType.MESH,
            )
        )
    for copy in scatter:
        copy.start()
    value = sent_ref[me]
    for step, copy in enumerate(scatter, 1):
        copy.wait_recv()
        value = value + parts[step]
    total[...] = value / n
    for copy in spread:
        copy.start()
    mean_ref[me] = total[...]
    for copy in scatter:
        copy.wait_send()
    for copy in spread:
        copy.wait()


def gather_rows(array, axis):
    n = lax.axis_size(axis)
    depth, cols = array.shape
    return pl.pallas_call(
        functools.partial(gather_kernel, axis, n),
        out_shape=jax.ShapeDtypeStruct((n * depth, cols), array.dtype),
        in_specs=[pl.BlockSpec(memory_space=pltpu.VMEM)],
        out_specs=pl.BlockSpec(memory_space=pl.ANY),
        scratch_shapes=[
            pltpu.SemaphoreType.DMA((n - 1, 2 * PIECES)),
            pltpu.SemaphoreType.DMA((n - 1, 2 * PIECES)),
            pltpu.SemaphoreType.DMA,
        ],
        compiler_params=pltpu.CompilerParams(collective_id=0, has_side_effects=True),
        name="gather_rows",
    )(array)


def mean_over(array, axis):
    n = lax.axis_size(axis)
    lanes = array.shape[-1]
    slices = array.reshape(n, -1, lanes)
    mean = pl.pallas_call(
        functools.partial(mean_kernel, axis, n),
        out_shape=jax.ShapeDtypeStruct(slices.shape, jnp.float32),
        in_specs=[pl.BlockSpec(memory_space=pltpu.VMEM)],
        out_specs=pl.BlockSpec(memory_space=pltpu.VMEM),
        scratch_shapes=[
            pltpu.VMEM(slices.shape, jnp.float32),
            pltpu.VMEM(slices.shape[1:], jnp.float32),
        ]
        + [pltpu.SemaphoreType.DMA((n,))] * 4,
        compiler_params=pltpu.CompilerParams(collective_id=1, has_side_effects=True),
        name="mean_over",
    )(slices)
    return mean.reshape(array.shape)


def body(inputs, out_grad, weight, momentum, selected):
    rows, cols = weight.shape
    tokens = inputs.shape[0]
    scale = 1.0 / math.sqrt(tokens)
    strips, steps = rows // BLK, cols // WIDE
    table = jnp.asarray(dct_table())
    gathered = gather_rows(out_grad, "tensor")
    turned = inputs.T
    picks = selected.reshape(strips, cols // LANES, LANES).swapaxes(0, 1)

    small = pl.BlockSpec((WIDE // LANES, strips, LANES), lambda c: (c, 0, 0))
    whole_table = pl.BlockSpec((BLK, LANES), lambda c: (0, 0))
    tall = pl.BlockSpec((rows, WIDE), lambda c: (0, c))
    fresh, sent = pl.pallas_call(
        functools.partial(momentum_kernel, scale, strips),
        grid=(steps,),
        out_shape=(
            jax.ShapeDtypeStruct((rows, cols), jnp.bfloat16),
            jax.ShapeDtypeStruct((cols // LANES, strips, LANES), jnp.float32),
        ),
        in_specs=[
            pl.BlockSpec((rows, tokens), lambda c: (0, 0)),
            pl.BlockSpec((tokens, WIDE), lambda c: (0, c)),
            tall,
            small,
            whole_table,
        ],
        out_specs=(tall, small),
        scratch_shapes=[pltpu.VMEM((rows, WIDE), jnp.float32)],
        cost_estimate=pl.CostEstimate(
            flops=2 * rows * cols * (tokens + 512), bytes_accessed=8 * rows * cols, transcendentals=0
        ),
        name="momentum_step",
    )(turned, gathered, momentum[0], picks, table)
    mean_sent = mean_over(sent, "replica")
    dacts = lax.dot_general(
        gathered, weight, (((1,), (1,)), ((), ())), preferred_element_type=jnp.float32
    ).astype(jnp.bfloat16)
    update = pl.pallas_call(
        functools.partial(update_kernel, strips),
        grid=(steps,),
        out_shape=jax.ShapeDtypeStruct((rows, cols), jnp.bfloat16),
        in_specs=[small, small, whole_table],
        out_specs=tall,
        cost_estimate=pl.CostEstimate(
            flops=2 * rows * cols * 256, bytes_accessed=2 * rows * cols, transcendentals=0
        ),
        name="update_step",
    )(mean_sent, picks, table)
    return dacts, fresh[None], update


def solution(mesh):
    return jax.shard_map(
        body,
        mesh=mesh,
        in_specs=(
            P("replica", "tensor"),
            P(("replica", "tensor"), None),
            P("tensor", None),
            P("replica", "tensor", None),
            P("tensor", None),
        ),
        out_specs=(P("replica", "tensor"), P("replica", "tensor", None), P("tensor", None)),
        check_vma=False,
    )
```

```python
import functools
import math

import jax
import jax.numpy as jnp
import numpy as np
from jax import lax
from jax.experimental import pallas as pl
from jax.experimental.pallas import tpu as pltpu
from jax.sharding import PartitionSpec as P

BLK = 64
TOPK = 64
LANES = 2 * BLK
WIDE = 256
LAG = 2


def dct_table():
    place = np.arange(BLK)[:, None]
    freq = np.arange(BLK)[None, :]
    table = np.cos(math.pi * (2.0 * place + 1.0) * freq / (2.0 * BLK)) * math.sqrt(2.0 / BLK)
    table[:, 0] = math.sqrt(1.0 / BLK)
    return np.concatenate([table, table], axis=1).astype(np.float32)


def split(x):
    high = x.astype(jnp.bfloat16)
    low = (x - high.astype(jnp.float32)).astype(jnp.bfloat16)
    return high, low


def bases(picks, table):
    rows_at = jnp.broadcast_to(lax.shift_right_logical(picks, 6), (BLK, LANES))
    cols_at = jnp.broadcast_to(picks & (BLK - 1), (BLK, LANES))
    row_basis = jnp.take_along_axis(table, rows_at, axis=1)
    col_basis = jnp.take_along_axis(table, cols_at, axis=1)
    first = lax.broadcasted_iota(jnp.int32, (BLK, LANES), 1) < BLK
    diagonal = jnp.concatenate(
        [jnp.where(first, col_basis, 0.0), jnp.where(first, 0.0, col_basis)], axis=0
    )
    return row_basis, split(diagonal)


def encode(block, row_basis, diagonal):
    high, low = split(block)
    dhigh, dlow = diagonal
    part = jnp.dot(
        jnp.concatenate([high, low], axis=0),
        jnp.concatenate([dhigh, dlow], axis=1),
        preferred_element_type=jnp.float32,
    )
    proj = part[:BLK, :LANES] + (part[:BLK, LANES:] + part[BLK:, :LANES])
    return jnp.sum(row_basis * proj, axis=0, keepdims=True)


def decode(values, row_basis, diagonal):
    high, low = split(row_basis * values)
    dhigh, dlow = diagonal
    part = lax.dot_general(
        jnp.concatenate([high, low], axis=0),
        jnp.concatenate([dhigh, dlow], axis=0),
        (((1,), (1,)), ((), ())),
        preferred_element_type=jnp.float32,
    )
    return part[:BLK, :LANES] + (part[:BLK, LANES:] + part[BLK:, :LANES])


def group_of(strips):
    return 8 if strips % 8 == 0 else strips


def momentum_kernel(
    axis, n, scale, strips, own_ref, x_ref, m_ref, w_ref, sel_ref, table_ref,
    fresh_ref, sent_ref, dacts_ref, acc_ref, all_ref, dacts_acc, send_sem, recv_sem,
):
    me = lax.axis_index(axis)
    right, left = lax.rem(me + 1, n), lax.rem(me + n - 1, n)
    depth = own_ref.shape[0]
    pieces = all_ref.shape[0] // 2
    turn = pl.program_id(0)

    def rows_of(owner):
        return pl.ds(pl.multiple_of(owner * depth, depth), depth)

    def hop(step, piece, way):
        chunk = way * pieces + piece
        owner = lax.rem(me + n - step, n) if way == 0 else lax.rem(me + step, n)
        there = all_ref.at[chunk, rows_of(owner)]
        return pltpu.make_async_remote_copy(
            src_ref=own_ref.at[:, pl.ds(chunk * WIDE, WIDE)] if step == 0 else there,
            dst_ref=there,
            send_sem=send_sem.at[step, chunk],
            recv_sem=recv_sem.at[step, chunk],
            device_id={axis: right if way == 0 else left},
            device_id_type=pl.DeviceIdType.MESH,
        )

    def forward(tick):
        for step in reversed(range(n - 1)):
            piece = tick - LAG * step
            if 0 <= piece < pieces:
                for way in range(2):
                    if step > 0:
                        hop(step - 1, piece, way).wait_recv()
                    hop(step, piece, way).start()

    ready = LAG * (n - 2) + 1

    @pl.when(turn == 0)
    def _():
        barrier = pltpu.get_barrier_semaphore()
        for peer in (left, right):
            pl.semaphore_signal(barrier, inc=1, device_id={axis: peer}, device_id_type=pl.DeviceIdType.MESH)
        pl.semaphore_wait(barrier, 2)
        for tick in range(ready):
            forward(tick)
            if tick == 0:
                for chunk in range(2 * pieces):
                    all_ref[chunk, rows_of(me)] = own_ref[:, pl.ds(chunk * WIDE, WIDE)]
                dacts_acc[...] = jnp.zeros_like(dacts_acc)

    for piece in range(pieces):
        @pl.when(turn == 2 * piece)
        def _():
            forward(piece + ready)
            for way in range(2):
                hop(n - 2, piece, way).wait_recv()

    @pl.when(turn == 2 * pieces - 1)
    def _():
        for step in range(n - 1):
            for piece in range(pieces):
                for way in range(2):
                    hop(step, piece, way).wait_send()

    grads = all_ref[lax.rem(turn, 2) * pieces + turn // 2]
    acc_ref[...] = (
        jnp.dot(x_ref[...], grads, preferred_element_type=jnp.float32) * scale
        + 0.999 * m_ref[...].astype(jnp.float32)
    )
    dacts_acc[...] += lax.dot_general(
        grads, w_ref[...], (((1,), (1,)), ((), ())), preferred_element_type=jnp.float32
    )

    @pl.when(turn == 2 * pieces - 1)
    def _():
        dacts_ref[...] = dacts_acc[...].astype(jnp.bfloat16)

    table = table_ref[...]

    some = group_of(strips)

    @pl.loop(0, strips // some)
    def _(group):
        near = pl.ds(pl.multiple_of(group * some, some), some)
        for pair in range(WIDE // LANES):
            lanes = pl.ds(pair * LANES, LANES)
            picks = sel_ref[pair, near]
            found = []
            for one in range(some):
                at = pl.ds(pl.multiple_of((group * some + one) * BLK, BLK), BLK)
                row_basis, diagonal = bases(picks[one : one + 1], table)
                block = acc_ref[at, lanes]
                values = encode(block, row_basis, diagonal)
                found.append(values)
                fresh_ref[at, lanes] = (block - decode(values, row_basis, diagonal)).astype(jnp.bfloat16)
            sent_ref[pair, near] = jnp.concatenate(found, axis=0)


def update_kernel(strips, mean_ref, sel_ref, table_ref, update_ref):
    table = table_ref[...]

    some = group_of(strips)

    @pl.loop(0, strips // some)
    def _(group):
        near = pl.ds(pl.multiple_of(group * some, some), some)
        for pair in range(WIDE // LANES):
            lanes = pl.ds(pair * LANES, LANES)
            picks = sel_ref[pair, near]
            means = mean_ref[pair, near] * (BLK / math.sqrt(TOPK))
            for one in range(some):
                at = pl.ds(pl.multiple_of((group * some + one) * BLK, BLK), BLK)
                row_basis, diagonal = bases(picks[one : one + 1], table)
                update_ref[at, lanes] = decode(means[one : one + 1], row_basis, diagonal).astype(jnp.bfloat16)


def greet(axis, n):
    me = lax.axis_index(axis)
    barrier = pltpu.get_barrier_semaphore()
    for step in range(1, n):
        pl.semaphore_signal(
            barrier, inc=1, device_id={axis: lax.rem(me + step, n)}, device_id_type=pl.DeviceIdType.MESH
        )
    pl.semaphore_wait(barrier, n - 1)
    return me


def mean_kernel(axis, n, sent_ref, mean_ref, parts, total, send_sem, recv_sem, back_sem, give_sem):
    me = greet(axis, n)
    scatter = []
    spread = []
    for step in range(1, n):
        peer = lax.rem(me + step, n)
        scatter.append(
            pltpu.make_async_remote_copy(
                src_ref=sent_ref.at[peer],
                dst_ref=parts.at[step],
                send_sem=send_sem.at[step],
                recv_sem=recv_sem.at[step],
                device_id={axis: peer},
                device_id_type=pl.DeviceIdType.MESH,
            )
        )
        spread.append(
            pltpu.make_async_remote_copy(
                src_ref=total,
                dst_ref=mean_ref.at[me],
                send_sem=back_sem.at[step],
                recv_sem=give_sem.at[step],
                device_id={axis: peer},
                device_id_type=pl.DeviceIdType.MESH,
            )
        )
    for copy in scatter:
        copy.start()
    value = sent_ref[me]
    for step, copy in enumerate(scatter, 1):
        copy.wait_recv()
        value = value + parts[step]
    total[...] = value / n
    for copy in spread:
        copy.start()
    mean_ref[me] = total[...]
    for copy in scatter:
        copy.wait_send()
    for copy in spread:
        copy.wait()


def mean_over(array, axis):
    n = lax.axis_size(axis)
    lanes = array.shape[-1]
    slices = array.reshape(n, -1, lanes)
    mean = pl.pallas_call(
        functools.partial(mean_kernel, axis, n),
        out_shape=jax.ShapeDtypeStruct(slices.shape, jnp.float32),
        in_specs=[pl.BlockSpec(memory_space=pltpu.VMEM)],
        out_specs=pl.BlockSpec(memory_space=pltpu.VMEM),
        scratch_shapes=[
            pltpu.VMEM(slices.shape, jnp.float32),
            pltpu.VMEM(slices.shape[1:], jnp.float32),
        ]
        + [pltpu.SemaphoreType.DMA((n,))] * 4,
        compiler_params=pltpu.CompilerParams(collective_id=1, has_side_effects=True),
        name="mean_over",
    )(slices)
    return mean.reshape(array.shape)


def body(inputs, out_grad, weight, momentum, selected):
    rows, cols = weight.shape
    tokens = inputs.shape[0]
    scale = 1.0 / math.sqrt(tokens)
    strips, steps = rows // BLK, cols // WIDE
    table = jnp.asarray(dct_table())
    n = lax.axis_size("tensor")
    turned = inputs.T
    picks = selected.reshape(strips, cols // LANES, LANES).swapaxes(0, 1)

    small = pl.BlockSpec((WIDE // LANES, strips, LANES), lambda c: (c, 0, 0))
    whole_table = pl.BlockSpec((BLK, LANES), lambda c: (0, 0))
    tall = pl.BlockSpec((rows, WIDE), lambda c: (0, c))
    half = steps // 2
    tall_turn = pl.BlockSpec((rows, WIDE), lambda c: (0, (c % 2) * half + c // 2))
    small_turn = pl.BlockSpec((WIDE // LANES, strips, LANES), lambda c: ((c % 2) * half + c // 2, 0, 0))
    fresh, sent, dacts = pl.pallas_call(
        functools.partial(momentum_kernel, "tensor", n, scale, strips),
        grid=(steps,),
        out_shape=(
            jax.ShapeDtypeStruct((rows, cols), jnp.bfloat16),
            jax.ShapeDtypeStruct((cols // LANES, strips, LANES), jnp.float32),
            jax.ShapeDtypeStruct((tokens, rows), jnp.bfloat16),
        ),
        in_specs=[
            pl.BlockSpec(out_grad.shape, lambda c: (0, 0)),
            pl.BlockSpec((rows, tokens), lambda c: (0, 0)),
            tall_turn,
            tall_turn,
            small_turn,
            whole_table,
        ],
        out_specs=(tall_turn, small_turn, pl.BlockSpec((tokens, rows), lambda c: (0, 0))),
        scratch_shapes=[
            pltpu.VMEM((rows, WIDE), jnp.float32),
            pltpu.VMEM((steps, tokens, WIDE), jnp.bfloat16),
            pltpu.VMEM((tokens, rows), jnp.float32),
            pltpu.SemaphoreType.DMA((n - 1, steps)),
            pltpu.SemaphoreType.DMA((n - 1, steps)),
        ],
        compiler_params=pltpu.CompilerParams(collective_id=0, has_side_effects=True),
        name="momentum_step",
    )(out_grad, turned, momentum[0], weight, picks, table)
    mean_sent = mean_over(sent, "replica")
    update = pl.pallas_call(
        functools.partial(update_kernel, strips),
        grid=(steps,),
        out_shape=jax.ShapeDtypeStruct((rows, cols), jnp.bfloat16),
        in_specs=[small, small, whole_table],
        out_specs=tall,
        cost_estimate=pl.CostEstimate(
            flops=2 * rows * cols * 256, bytes_accessed=2 * rows * cols, transcendentals=0
        ),
        name="update_step",
    )(mean_sent, picks, table)
    return dacts, fresh[None], update


def solution(mesh):
    return jax.shard_map(
        body,
        mesh=mesh,
        in_specs=(
            P("replica", "tensor"),
            P(("replica", "tensor"), None),
            P("tensor", None),
            P("replica", "tensor", None),
            P("tensor", None),
        ),
        out_specs=(P("replica", "tensor"), P("replica", "tensor", None), P("tensor", None)),
        check_vma=False,
    )
```

```python
import functools
import math

import jax
import jax.numpy as jnp
import numpy as np
from jax import lax
from jax.experimental import pallas as pl
from jax.experimental.pallas import tpu as pltpu
from jax.sharding import PartitionSpec as P

BLK = 64
TOPK = 64
LANES = 2 * BLK
WIDE = 256
LAG = 2


def dct_table():
    place = np.arange(BLK)[:, None]
    freq = np.arange(BLK)[None, :]
    table = np.cos(math.pi * (2.0 * place + 1.0) * freq / (2.0 * BLK)) * math.sqrt(2.0 / BLK)
    table[:, 0] = math.sqrt(1.0 / BLK)
    return np.concatenate([table, table], axis=1).astype(np.float32)


def split(x):
    high = x.astype(jnp.bfloat16)
    low = (x - high.astype(jnp.float32)).astype(jnp.bfloat16)
    return high, low


def bases(picks, table):
    rows_at = jnp.broadcast_to(lax.shift_right_logical(picks, 6), (BLK, LANES))
    cols_at = jnp.broadcast_to(picks & (BLK - 1), (BLK, LANES))
    row_basis = jnp.take_along_axis(table, rows_at, axis=1)
    col_basis = jnp.take_along_axis(table, cols_at, axis=1)
    first = lax.broadcasted_iota(jnp.int32, (BLK, LANES), 1) < BLK
    diagonal = jnp.concatenate(
        [jnp.where(first, col_basis, 0.0), jnp.where(first, 0.0, col_basis)], axis=0
    )
    return row_basis, split(diagonal)


def encode(block, row_basis, diagonal):
    high, low = split(block)
    dhigh, dlow = diagonal
    part = jnp.dot(
        jnp.concatenate([high, low], axis=0),
        jnp.concatenate([dhigh, dlow], axis=1),
        preferred_element_type=jnp.float32,
    )
    proj = part[:BLK, :LANES] + (part[:BLK, LANES:] + part[BLK:, :LANES])
    return jnp.sum(row_basis * proj, axis=0, keepdims=True)


def decode(values, row_basis, diagonal):
    high, low = split(row_basis * values)
    dhigh, dlow = diagonal
    part = lax.dot_general(
        jnp.concatenate([high, low], axis=0),
        jnp.concatenate([dhigh, dlow], axis=0),
        (((1,), (1,)), ((), ())),
        preferred_element_type=jnp.float32,
    )
    return part[:BLK, :LANES] + (part[:BLK, LANES:] + part[BLK:, :LANES])


def group_of(strips):
    return 8 if strips % 8 == 0 else strips


def momentum_kernel(
    axis, n, scale, strips, own_ref, x_ref, m_ref, w_ref, sel_ref, table_ref,
    fresh_ref, sent_ref, dacts_ref, acc_ref, all_ref, dacts_acc, send_sem, recv_sem,
):
    me = lax.axis_index(axis)
    right, left = lax.rem(me + 1, n), lax.rem(me + n - 1, n)
    depth = own_ref.shape[0]
    pieces = all_ref.shape[0] // 2
    turn = pl.program_id(0)

    def rows_of(owner):
        return pl.ds(pl.multiple_of(owner * depth, depth), depth)

    def hop(step, piece, way):
        chunk = way * pieces + piece
        owner = lax.rem(me + n - step, n) if way == 0 else lax.rem(me + step, n)
        there = all_ref.at[chunk, rows_of(owner)]
        return pltpu.make_async_remote_copy(
            src_ref=own_ref.at[:, pl.ds(chunk * WIDE, WIDE)] if step == 0 else there,
            dst_ref=there,
            send_sem=send_sem.at[step, chunk],
            recv_sem=recv_sem.at[step, chunk],
            device_id={axis: right if way == 0 else left},
            device_id_type=pl.DeviceIdType.MESH,
        )

    def forward(tick):
        for step in reversed(range(n - 1)):
            piece = tick - LAG * step
            if 0 <= piece < pieces:
                for way in range(2):
                    if step > 0:
                        hop(step - 1, piece, way).wait_recv()
                    hop(step, piece, way).start()

    ready = LAG * (n - 2) + 1

    @pl.when(turn == 0)
    def _():
        barrier = pltpu.get_barrier_semaphore()
        for peer in (left, right):
            pl.semaphore_signal(barrier, inc=1, device_id={axis: peer}, device_id_type=pl.DeviceIdType.MESH)
        pl.semaphore_wait(barrier, 2)
        for tick in range(ready):
            forward(tick)
            if tick == 0:
                for chunk in range(2 * pieces):
                    all_ref[chunk, rows_of(me)] = own_ref[:, pl.ds(chunk * WIDE, WIDE)]
                dacts_acc[...] = jnp.zeros_like(dacts_acc)

    for piece in range(pieces):
        @pl.when(turn == 2 * piece)
        def _():
            forward(piece + ready)
            for way in range(2):
                hop(n - 2, piece, way).wait_recv()

    @pl.when(turn == 2 * pieces - 1)
    def _():
        for step in range(n - 1):
            for piece in range(pieces):
                for way in range(2):
                    hop(step, piece, way).wait_send()

    grads = all_ref[lax.rem(turn, 2) * pieces + turn // 2]
    acc_ref[...] = (
        jnp.dot(x_ref[...], grads, preferred_element_type=jnp.float32) * scale
        + 0.999 * m_ref[...].astype(jnp.float32)
    )
    dacts_acc[...] += lax.dot_general(
        grads, w_ref[...], (((1,), (1,)), ((), ())), preferred_element_type=jnp.float32
    )

    @pl.when(turn == 2 * pieces - 1)
    def _():
        dacts_ref[...] = dacts_acc[...].astype(jnp.bfloat16)

    table = table_ref[...]

    some = group_of(strips)

    @pl.loop(0, strips // some)
    def _(group):
        near = pl.ds(pl.multiple_of(group * some, some), some)
        for pair in range(WIDE // LANES):
            lanes = pl.ds(pair * LANES, LANES)
            picks = sel_ref[pair, near]
            found = []
            for one in range(some):
                at = pl.ds(pl.multiple_of((group * some + one) * BLK, BLK), BLK)
                row_basis, diagonal = bases(picks[one : one + 1], table)
                block = acc_ref[at, lanes]
                values = encode(block, row_basis, diagonal)
                found.append(values)
                fresh_ref[at, lanes] = (block - decode(values, row_basis, diagonal)).astype(jnp.bfloat16)
            sent_ref[pair, near] = jnp.concatenate(found, axis=0)


def update_kernel(strips, mean_ref, sel_ref, table_ref, held_ref, update_ref, fresh_ref):
    fresh_ref[...] = held_ref[...]
    table = table_ref[...]

    some = group_of(strips)

    @pl.loop(0, strips // some)
    def _(group):
        near = pl.ds(pl.multiple_of(group * some, some), some)
        for pair in range(WIDE // LANES):
            lanes = pl.ds(pair * LANES, LANES)
            picks = sel_ref[pair, near]
            means = mean_ref[pair, near] * (BLK / math.sqrt(TOPK))
            for one in range(some):
                at = pl.ds(pl.multiple_of((group * some + one) * BLK, BLK), BLK)
                row_basis, diagonal = bases(picks[one : one + 1], table)
                update_ref[at, lanes] = decode(means[one : one + 1], row_basis, diagonal).astype(jnp.bfloat16)


def greet(axis, n):
    me = lax.axis_index(axis)
    barrier = pltpu.get_barrier_semaphore()
    for step in range(1, n):
        pl.semaphore_signal(
            barrier, inc=1, device_id={axis: lax.rem(me + step, n)}, device_id_type=pl.DeviceIdType.MESH
        )
    pl.semaphore_wait(barrier, n - 1)
    return me


def mean_kernel(axis, n, sent_ref, mean_ref, parts, total, send_sem, recv_sem, back_sem, give_sem):
    me = greet(axis, n)
    scatter = []
    spread = []
    for step in range(1, n):
        peer = lax.rem(me + step, n)
        scatter.append(
            pltpu.make_async_remote_copy(
                src_ref=sent_ref.at[peer],
                dst_ref=parts.at[step],
                send_sem=send_sem.at[step],
                recv_sem=recv_sem.at[step],
                device_id={axis: peer},
                device_id_type=pl.DeviceIdType.MESH,
            )
        )
        spread.append(
            pltpu.make_async_remote_copy(
                src_ref=total,
                dst_ref=mean_ref.at[me],
                send_sem=back_sem.at[step],
                recv_sem=give_sem.at[step],
                device_id={axis: peer},
                device_id_type=pl.DeviceIdType.MESH,
            )
        )
    for copy in scatter:
        copy.start()
    value = sent_ref[me]
    for step, copy in enumerate(scatter, 1):
        copy.wait_recv()
        value = value + parts[step]
    total[...] = value / n
    for copy in spread:
        copy.start()
    mean_ref[me] = total[...]
    for copy in scatter:
        copy.wait_send()
    for copy in spread:
        copy.wait()


def mean_over(array, axis):
    n = lax.axis_size(axis)
    lanes = array.shape[-1]
    slices = array.reshape(n, -1, lanes)
    mean = pl.pallas_call(
        functools.partial(mean_kernel, axis, n),
        out_shape=jax.ShapeDtypeStruct(slices.shape, jnp.float32),
        in_specs=[pl.BlockSpec(memory_space=pltpu.VMEM)],
        out_specs=pl.BlockSpec(memory_space=pltpu.VMEM),
        scratch_shapes=[
            pltpu.VMEM(slices.shape, jnp.float32),
            pltpu.VMEM(slices.shape[1:], jnp.float32),
        ]
        + [pltpu.SemaphoreType.DMA((n,))] * 4,
        compiler_params=pltpu.CompilerParams(collective_id=1, has_side_effects=True),
        name="mean_over",
    )(slices)
    return mean.reshape(array.shape)


def body(inputs, out_grad, weight, momentum, selected):
    rows, cols = weight.shape
    tokens = inputs.shape[0]
    scale = 1.0 / math.sqrt(tokens)
    strips, steps = rows // BLK, cols // WIDE
    table = jnp.asarray(dct_table())
    n = lax.axis_size("tensor")
    turned = inputs.T
    picks = selected.reshape(strips, cols // LANES, LANES).swapaxes(0, 1)

    small = pl.BlockSpec((WIDE // LANES, strips, LANES), lambda c: (c, 0, 0))
    whole_table = pl.BlockSpec((BLK, LANES), lambda c: (0, 0))
    tall = pl.BlockSpec((rows, WIDE), lambda c: (0, c))
    half = steps // 2
    tall_turn = pl.BlockSpec((rows, WIDE), lambda c: (0, (c % 2) * half + c // 2))
    small_turn = pl.BlockSpec((WIDE // LANES, strips, LANES), lambda c: ((c % 2) * half + c // 2, 0, 0))
    fresh, sent, dacts = pl.pallas_call(
        functools.partial(momentum_kernel, "tensor", n, scale, strips),
        grid=(steps,),
        out_shape=(
            jax.ShapeDtypeStruct((rows, cols), jnp.bfloat16),
            jax.ShapeDtypeStruct((cols // LANES, strips, LANES), jnp.float32),
            jax.ShapeDtypeStruct((tokens, rows), jnp.bfloat16),
        ),
        in_specs=[
            pl.BlockSpec(out_grad.shape, lambda c: (0, 0)),
            pl.BlockSpec((rows, tokens), lambda c: (0, 0)),
            tall_turn,
            tall_turn,
            small_turn,
            whole_table,
        ],
        out_specs=(tall_turn, small_turn, pl.BlockSpec((tokens, rows), lambda c: (0, 0))),
        scratch_shapes=[
            pltpu.VMEM((rows, WIDE), jnp.float32),
            pltpu.VMEM((steps, tokens, WIDE), jnp.bfloat16),
            pltpu.VMEM((tokens, rows), jnp.float32),
            pltpu.SemaphoreType.DMA((n - 1, steps)),
            pltpu.SemaphoreType.DMA((n - 1, steps)),
        ],
        compiler_params=pltpu.CompilerParams(collective_id=0, has_side_effects=True),
        name="momentum_step",
    )(out_grad, turned, momentum[0], weight, picks, table)
    mean_sent = mean_over(sent, "replica")
    update, fresh = pl.pallas_call(
        functools.partial(update_kernel, strips),
        grid=(steps,),
        out_shape=(jax.ShapeDtypeStruct((rows, cols), jnp.bfloat16),) * 2,
        in_specs=[small, small, whole_table, tall],
        out_specs=(tall, tall),
        cost_estimate=pl.CostEstimate(
            flops=2 * rows * cols * 256, bytes_accessed=2 * rows * cols, transcendentals=0
        ),
        name="update_step",
    )(mean_sent, picks, table, fresh)
    return dacts, fresh[None], update


def solution(mesh):
    return jax.shard_map(
        body,
        mesh=mesh,
        in_specs=(
            P("replica", "tensor"),
            P(("replica", "tensor"), None),
            P("tensor", None),
            P("replica", "tensor", None),
            P("tensor", None),
        ),
        out_specs=(P("replica", "tensor"), P("replica", "tensor", None), P("tensor", None)),
        check_vma=False,
    )
```
